256 devices in a mesh: section: 16 (over z_lo, x), ctx: 16 (over z_hi, y, core).
Axes of the slice: x: 4, y: 4, z: 8 (z_hi: 2, z_lo: 4; z = z_hi * 4 + z_lo), core: 2. Of those that a mesh axis runs over, the one named last changes fastest.
Arguments:
- queries: bfloat16 [16, 4096, 16, 128], P('section', 'ctx'), may hold values from -12 to 12
- keys: bfloat16 [16, 4096, 128], P('section', 'ctx'), may hold values from -6 to 6
- values: bfloat16 [16, 4096, 128], P('section', 'ctx'), may hold values from -6 to 6
- outputs: bfloat16 [16, 4096, 16, 128], P('section', 'ctx'), may hold values from -6 to 6, as said below
- grad_held: bfloat16 [16, 4096, 16, 128], P('section', 'ctx'), may hold values from -24 to 24
- lse: float32 [16, 16, 4096], P('section', None, 'ctx'), as said below
- span_start: int32 [32], replicated, may hold values from 0 to 3968, as said below
Outputs:
- query_grad: bfloat16 [16, 4096, 16, 128], P('section', 'ctx')
- key_grad: bfloat16 [16, 4096, 128], P('section', 'ctx')
- value_grad: bfloat16 [16, 4096, 128], P('section', 'ctx')
The draws below stay inside these ranges and needn't reach their ends.
Inputs may be any that keep to these rules, and one draw needn't show every extreme that they name: `span_start`: each multiple of 128 below 4096 appears once. Entries 2 k and 2 k + 1 are the spans held by index k of ctx; they add up to 3968, the smaller first. lse[s, h, i] is the log of the sum of exp(scores[s, h, i, j]) over the j with positions[j] <= positions[i]. outputs[s, i, h] is the sum over j of probs[s, h, i, j] values[s, j], rounded once.
All inputs are finite; a program needn't handle non-finite values.
Results may differ from the reference program's by a relative error of at most 0.014.
Values may be sent and summed in bfloat16 or wider, within the bound.
A program may use at most 64 MiB of HBM per device.

```python
import jax
import jax.numpy as jnp
from jax import lax

HQ = 16
HD = 128
TOK_DEV = 256
SECTIONS = 16
SPANS = 32
CH = 128
SEQ = 4096
N_CTX = 16


def span_layout(key):
    order = jax.random.permutation(jax.random.fold_in(key, 11), SPANS // 2)
    lower_start = order * CH
    upper_start = (SPANS - 1 - order) * CH
    return jnp.stack([lower_start, upper_start], axis=1).reshape(SPANS).astype(jnp.int32)


def draw_span_start(key, part):
    return span_layout(key)


def draw_queries(key, part):
    key_values = jax.random.fold_in(jax.random.fold_in(key, 21), 0)
    full_shape = (SECTIONS, SEQ, HQ, HD)
    result = 2.0 * jax.random.normal(key_values, full_shape, jnp.float32)
    return jnp.clip(result, -12.0, 12.0).astype(jnp.bfloat16)


def draw_keys(key, part):
    key_values = jax.random.fold_in(jax.random.fold_in(key, 22), 0)
    full_shape = (SECTIONS, SEQ, HD)
    result = jax.random.normal(key_values, full_shape, jnp.float32)
    return jnp.clip(result, -6.0, 6.0).astype(jnp.bfloat16)


def draw_values(key, part):
    key_values = jax.random.fold_in(jax.random.fold_in(key, 23), 0)
    full_shape = (SECTIONS, SEQ, HD)
    result = jax.random.normal(key_values, full_shape, jnp.float32)
    return jnp.clip(result, -6.0, 6.0).astype(jnp.bfloat16)


def attention_forward(key, part):
    all_queries = draw_queries(key, part).astype(jnp.float32)
    all_keys = draw_keys(key, part).astype(jnp.float32)
    all_values = draw_values(key, part).astype(jnp.float32)
    starts = span_layout(key)
    positions = (starts[:, None] + jnp.arange(CH, dtype=jnp.int32)[None, :]).reshape(SEQ)
    score_scale = HD ** (-0.5)
    blocks = SPANS // 2

    def one_section(section_items):
        section_q, section_k, section_v = section_items

        def one_block(block_items):
            block_q, block_pos = block_items
            scores = jnp.einsum('rhd,cd->hrc', block_q, section_k, precision=lax.Precision.HIGHEST) * score_scale
            allowed = positions[None, None, :] <= block_pos[None, :, None]
            scores = jnp.where(allowed, scores, -jnp.inf)
            block_lse = jax.scipy.special.logsumexp(scores, axis=-1)
            probs = jnp.where(allowed, jnp.exp(scores - block_lse[:, :, None]), 0.0)
            block_out = jnp.einsum('hrc,cd->rhd', probs, section_v, precision=lax.Precision.HIGHEST)
            return (block_lse, block_out)
        block_lse, block_out = lax.map(one_block, (section_q.reshape(blocks, TOK_DEV, HQ, HD), positions.reshape(blocks, TOK_DEV)))
        return (block_lse.transpose(1, 0, 2).reshape(HQ, SEQ), block_out.reshape(SEQ, HQ, HD))
    return lax.map(one_section, (all_queries, all_keys, all_values))


def draw_lse(key, part):
    return attention_forward(key, part)[0]


def draw_outputs(key, part):
    return jnp.clip(attention_forward(key, part)[1], -6.0, 6.0).astype(jnp.bfloat16)


def shard_levels(key, shape, pieces, low, top_value):
    level = 1.0
    for dim, blocks in pieces:
        steps = jax.random.uniform(jax.random.fold_in(jax.random.fold_in(key, 6), dim), (blocks,), jnp.float32, low / len(pieces), top_value / len(pieces))
        level = level * jnp.repeat(jnp.exp(steps), shape[dim] // blocks).reshape((-1,) + (1,) * (len(shape) - 1 - dim))
    return level


def noise(own_key, dims, scale, bound, cuts=(), kind=jnp.bfloat16):
    values = jax.random.normal(own_key, dims, jnp.float32) * scale
    if len(cuts) > 0:
        values = shard_levels(own_key, dims, cuts, -0.22, 0.18) * values
    return jnp.clip(values, min=-bound, max=bound).astype(kind)


def setup_inputs(seed: int = 0) -> dict:
    key_of = jax.random.split(jax.random.key(seed), 8)
    queries = draw_queries(jax.random.fold_in(key_of[7], 71), 0)
    keys = draw_keys(jax.random.fold_in(key_of[7], 71), 0)
    values = draw_values(jax.random.fold_in(key_of[7], 71), 0)
    outputs = draw_outputs(jax.random.fold_in(key_of[7], 71), 0)
    grad_held = noise(key_of[4], (SECTIONS, SEQ, HQ, HD), 4.0, 24.0, ((0, 16), (1, 16)))
    lse = draw_lse(jax.random.fold_in(key_of[7], 71), 0)
    span_start = draw_span_start(jax.random.fold_in(key_of[7], 71), 0)
    return dict(queries=queries, keys=keys, values=values, outputs=outputs, grad_held=grad_held, lse=lse, span_start=span_start)


def block_reference(query_rows, grad_rows, lse_rows, delta_rows, query_pos, key_rows, value_rows, key_pos):
    score_scale = HD ** -0.5
    query_float = query_rows.astype(jnp.float32)
    grad_float = grad_rows.astype(jnp.float32)
    key_float = key_rows.astype(jnp.float32)
    value_float = value_rows.astype(jnp.float32)
    highest = lax.Precision.HIGHEST
    scores = jnp.einsum("rhd,cd->hrc", query_float, key_float, precision=highest) * score_scale
    allowed = key_pos[None, :] <= query_pos[:, None]
    probs = jnp.where(allowed[None], jnp.exp(scores - lse_rows[:, :, None]), 0.0)
    probs_low = lax.optimization_barrier(probs.astype(jnp.bfloat16)).astype(jnp.float32)
    grad_probs = jnp.einsum("rhd,cd->hrc", grad_float, value_float, precision=highest)
    grad_scores = lax.optimization_barrier((probs * (grad_probs - delta_rows[:, :, None])).astype(jnp.bfloat16)).astype(jnp.float32)
    query_grad = jnp.einsum("hrc,cd->rhd", grad_scores, key_float, precision=highest) * score_scale
    key_grad = jnp.einsum("hrc,rhd->cd", grad_scores, query_float, precision=highest) * score_scale
    value_grad = jnp.einsum("hrc,rhd->cd", probs_low, grad_float, precision=highest)
    return query_grad, key_grad, value_grad


def reference(queries, keys, values, outputs, grad_held, lse, span_start):
    positions = (span_start[:, None] + jnp.arange(CH, dtype=jnp.int32)[None, :]).reshape(SEQ).astype(jnp.int32)
    grad_next = jnp.roll(grad_held, -1, axis=0)

    def one_section(section_items):
        section_q, section_k, section_v, section_o, section_g, section_lse = section_items
        delta_rows = jnp.sum(section_g.astype(jnp.float32) * section_o.astype(jnp.float32), axis=-1).T
        blocks = N_CTX
        block_items = (
            section_q.reshape(blocks, TOK_DEV, HQ, HD),
            section_g.reshape(blocks, TOK_DEV, HQ, HD),
            section_lse.reshape(HQ, blocks, TOK_DEV).transpose(1, 0, 2),
            delta_rows.reshape(HQ, blocks, TOK_DEV).transpose(1, 0, 2),
            positions.reshape(blocks, TOK_DEV),
        )

        def block_step(totals, scan_items):
            block_q, block_g, block_lse, block_delta, block_pos = scan_items
            query_grad, key_grad, value_grad = block_reference(block_q, block_g, block_lse, block_delta, block_pos, section_k, section_v, positions)
            return (totals[0] + key_grad, totals[1] + value_grad), query_grad.astype(jnp.bfloat16)

        zero_rows = jnp.zeros((SEQ, HD), jnp.float32)
        (key_total, value_total), query_blocks = lax.scan(block_step, (zero_rows, zero_rows), block_items)
        return query_blocks.reshape(SEQ, HQ, HD), key_total.astype(jnp.bfloat16), value_total.astype(jnp.bfloat16)

    query_grad, key_grad, value_grad = lax.map(one_section, (queries, keys, values, outputs, grad_next, lse))
    return query_grad, key_grad, value_grad
```

```python
import jax
import jax.numpy as jnp
from jax import lax
from jax.experimental import pallas as pl
from jax.experimental.pallas import tpu as pltpu
from jax.sharding import PartitionSpec as P

bf16, f32 = jnp.bfloat16, jnp.float32
LOG2E = 1.4426950408889634
FAR = 1e30
MESH = pl.DeviceIdType.MESH
PHASES = 2


def nn(a, b):
    return lax.dot_general(a, b, (((1,), (0,)), ((), ())), preferred_element_type=f32)


def nt(a, b):
    return lax.dot_general(a, b, (((1,), (1,)), ((), ())), preferred_element_type=f32)


def pair(top_left, top_right, bottom_left, bottom_right):
    top = jnp.concatenate([top_left, top_right], 1)
    return jnp.concatenate([top, jnp.concatenate([bottom_left, bottom_right], 1)], 0)


def attend(key_pair, value_pair, lse_pair, delta_pair, mask, rows, qc, dc, dq):
    span = key_pair.shape[0] // 2
    scale2 = (key_pair.shape[1] // 2) ** -0.5 * LOG2E
    scores = nt(key_pair, qc[rows, :]) * scale2
    grads = nt(value_pair, dc[rows, :])
    probs, terms = [], []
    for slot in range(2):
        part = slice(slot * span, (slot + 1) * span)
        prob = jnp.exp2(scores[part] - lse_pair[slot])
        if mask is not None:
            prob = jnp.where(mask, prob, 0.0)
        probs.append(prob)
        terms.append(prob * (grads[part] - delta_pair[slot]))
    probs = jnp.concatenate(probs, 0).astype(bf16)
    terms = jnp.concatenate(terms, 0).astype(bf16)
    dq[:, rows] += nn(key_pair.T, terms)
    return nn(terms, qc[rows, :]), nn(probs, dc[rows, :])


def kernel(
    starts, q, k, v, g, o, lse, dq_out, dk_out, dv_out,
    qc, dc, ob, lb, kv, dq, lse_rows, delta, acc, cred, send1, send2, yred, zsend, zred,
    in_s, grad_s, grad_r, kv_s, kv_r, fwd_s, s1_s, s1_r, s2_s, s2_r, z_s, z_r,
):
    me, sec = lax.axis_index("ctx"), lax.axis_index("section")
    sections = lax.axis_size("section")
    half_rows, head = qc.shape[0], qc.shape[1] // 2
    span = kv.shape[1] // 2
    scale = head ** -0.5
    step = half_rows // PHASES
    zh, y, core = me // 8, (me // 2) % 4, me % 2

    def at(dz, dy, dc):
        return (((zh + dz) % 2) * 4 + (y + dy) % 4) * 2 + (core + dc) % 2

    def index_of(j):
        return at(j // 8, j % 4, (j // 4) % 2)

    def remote(src, dst, send, recv, target):
        return pltpu.make_async_remote_copy(
            src_ref=src, dst_ref=dst, send_sem=send, recv_sem=recv,
            device_id=target, device_id_type=MESH,
        )

    core_peer, z_peer = {"ctx": at(0, 0, 1)}, {"ctx": at(1, 0, 0)}
    y_peers = [{"ctx": at(0, dy, 0)} for dy in (1, 2, 3)]
    before = {"section": (sec + sections - 1) % sections}
    after = {"section": (sec + 1) % sections}

    local = [
        pltpu.make_async_copy(k, kv.at[me, :, pl.ds(0, head)], in_s.at[0]),
        pltpu.make_async_copy(v, kv.at[me, :, pl.ds(head, head)], in_s.at[1]),
        pltpu.make_async_copy(lse, lb, in_s.at[2]),
    ]
    for half in range(2):
        part, cols = pl.ds(half * half_rows, half_rows), pl.ds(half * head, head)
        local.append(pltpu.make_async_copy(q.at[part, :], qc.at[:, cols], in_s.at[3 + half]))
        local.append(pltpu.make_async_copy(o.at[part, :], ob.at[:, cols], in_s.at[5 + half]))
    for copy in local:
        copy.start()

    barrier = pltpu.get_barrier_semaphore()
    peers = [core_peer, z_peer, *y_peers, before, after]
    for peer in peers:
        pl.semaphore_signal(barrier, inc=1, device_id=peer, device_id_type=MESH)
    pl.semaphore_wait(barrier, len(peers))

    grads = []
    for phase in range(PHASES):
        for half in range(2):
            n = phase * 2 + half
            grads.append(
                remote(
                    g.at[pl.ds(half * half_rows + phase * step, step), :],
                    dc.at[pl.ds(phase * step, step), pl.ds(half * head, head)],
                    grad_s.at[n], grad_r.at[n], before,
                )
            )
            grads[-1].start()
    for copy in local[:2]:
        copy.wait()

    def spread(shard, base, first):
        out = []
        for n, (peer, slot) in enumerate(
            [(y_peers[0], 3), (y_peers[2], 1), (y_peers[1], 2), (core_peer, 4)]
        ):
            out.append(
                remote(kv.at[shard], kv.at[shard], kv_s.at[base + n], kv_r.at[first + slot], peer)
            )
            out[-1].start()
        return out

    def arrived(j):
        spot = kv.at[index_of(j)]
        remote(spot, spot, kv_s.at[0], kv_r.at[j], core_peer).wait_recv()

    def forward(j):
        spot = kv.at[index_of(j)]
        return remote(spot, spot, fwd_s.at[j], kv_r.at[j + 4], core_peer)

    z_copy = remote(kv.at[me], kv.at[me], kv_s.at[8], kv_r.at[8], z_peer)
    z_copy.start()
    kv_copies = [z_copy, *spread(me, 0, 0)]

    dq[...] = jnp.zeros_like(dq)
    for copy in local[2:]:
        copy.wait()
    lane = lax.broadcasted_iota(jnp.int32, (16, 128), 1)
    pick = jnp.where(lane % 16 == lax.broadcasted_iota(jnp.int32, (16, 128), 0), 1.0, 0.0).astype(f32)
    tokens = lax.broadcasted_iota(jnp.int32, (128, 128), 0)
    lanes = lax.broadcasted_iota(jnp.int32, (128, 128), 1)
    for half in range(2):
        part = lb[:, half * 128 : (half + 1) * 128] * LOG2E
        wide = lax.dot_general(
            part, pick, (((0,), (0,)), ((), ())),
            precision=lax.Precision.HIGHEST, preferred_element_type=f32,
        )
        wide = jnp.where(lanes // 16 == tokens % 8, wide, 0.0)
        packed = jnp.sum(wide.reshape(16, 8, 128), axis=1)
        for i in range(16):
            lse_rows[half, :, i * 128 : (i + 1) * 128] = packed[i : i + 1]

    for j in (1, 3, 2):
        arrived(j)
        forward(j).start()
    arrived(8)
    kv_copies += spread(index_of(8), 4, 8)

    zero = jnp.zeros((span, head), bf16)
    low_start = starts[2 * me]
    ones = jnp.ones((8, head), bf16)

    def rows_of(phase):
        return pl.ds(phase * step, step)

    def start_phase(phase):
        rows = rows_of(phase)
        for half in range(2):
            grads[phase * 2 + half].wait_recv()
        for half in range(2):
            cols = pl.ds(half * head, head)
            prod = dc[rows, cols].astype(f32) * ob[rows, cols].astype(f32)
            high = prod.astype(bf16)
            low = (prod - high.astype(f32)).astype(bf16)
            delta[half, :, rows] = (nt(ones, high) + nt(ones, low))[:1]

    def diagonal(phase):
        rows = rows_of(phase)
        token = lax.shift_right_logical(
            lax.broadcasted_iota(jnp.int32, (span, step), 1), (half_rows // span).bit_length() - 1
        ) + phase * (step * span // half_rows)
        mask = lax.broadcasted_iota(jnp.int32, (span, step), 0) <= token
        k_a, k_b = kv[me, :span, :head], kv[me, span:, :head]
        v_a, v_b = kv[me, :span, head:], kv[me, span:, head:]
        dk, dv = attend(
            pair(zero, k_b, k_a, zero),
            pair(zero, v_b, v_a, zero),
            (lse_rows[1, :, rows], lse_rows[0, :, rows]),
            (delta[1, :, rows], delta[0, :, rows]),
            mask, rows, qc, dc, dq,
        )
        dk *= scale
        return pair(dk[span:, :head], dv[span:, :head], dk[:span, head:], dv[:span, head:])

    def shard_terms(j, phase):
        rows = rows_of(phase)
        m = index_of(j)
        sel = starts[2 * m] < low_start
        on = jnp.where(sel, 1.0, 0.0).astype(f32)
        off = 1.0 - on
        lse_a, lse_b = lse_rows[0, :, rows], lse_rows[1, :, rows]
        del_a, del_b = delta[0, :, rows], delta[1, :, rows]
        k_a, k_b = kv[m, :span, :head], kv[m, span:, :head]
        v_a, v_b = kv[m, :span, head:], kv[m, span:, head:]
        dk, dv = attend(
            pair(zero, k_a, (k_a * on).astype(bf16), (k_b * off).astype(bf16)),
            pair(zero, v_a, (v_a * on).astype(bf16), (v_b * off).astype(bf16)),
            (lse_b, jnp.where(j == 0, FAR, jnp.where(sel, lse_a, lse_b))),
            (del_b, jnp.where(sel, del_a, del_b)),
            None, rows, qc, dc, dq,
        )
        dk *= scale
        return pair(
            dk[:span, head:] + on * dk[span:, :head],
            dv[:span, head:] + on * dv[span:, :head],
            off * dk[span:, head:],
            off * dv[span:, head:],
        )

    def finish_rows(phase):
        for half in range(2):
            part = dq[half * head : (half + 1) * head, phase * step : (phase + 1) * step]
            dq_out[pl.ds(half * half_rows + phase * step, step), :] = (part.T * scale).astype(bf16)

    start_phase(0)
    acc[0] = diagonal(0)

    def first(j, carry):
        waits = jnp.logical_or(j // 4 == 1, j >= 9)

        @pl.when(waits)
        def _():
            arrived(j)

        @pl.when(jnp.logical_and(j >= 9, j < 12))
        def _():
            forward(j).start()

        terms = shard_terms(j, 0)

        @pl.when(j == 0)
        def _():
            acc[0] += terms

        @pl.when(j > 0)
        def _():
            acc[j] = terms

        return carry

    lax.fori_loop(0, 16, first, 0)
    finish_rows(0)
    start_phase(1)

    def sum1(n):
        return remote(send1.at[n], cred.at[n], s1_s.at[n], s1_r.at[n], core_peer)

    def sum2(n):
        dy = n % 4
        back = (n // 4) * 4 + (4 - dy) % 4
        return remote(
            send2.at[n], yred.at[back], s2_s.at[n], s2_r.at[back], {"ctx": at(0, dy, 0)}
        )

    def got2(n):
        remote(send2.at[n], yred.at[n], s2_s.at[n], s2_r.at[n], core_peer).wait_recv()

    z_sum = remote(zsend, zred, z_s.at[0], z_r.at[0], z_peer)

    def second(i, carry):
        j = 15 - i
        n = (j // 8) * 4 + j % 4
        terms = acc[j] + shard_terms(j, 1)
        kept = (j // 4) % 2 == 0

        @pl.when(jnp.logical_not(kept))
        def _():
            send1[n] = terms.astype(bf16)
            sum1(n).start()

        @pl.when(kept)
        def _():
            sum1(n).wait_recv()
            total = terms + cred[n].astype(f32)

            @pl.when(j % 4 == 0)
            def _():
                acc[j] = total

            @pl.when(j % 4 != 0)
            def _():
                send2[n] = total.astype(bf16)
                sum2(n).start()

        @pl.when(j == 5)
        def _():
            total = acc[8]
            for dy in (1, 2, 3):
                got2(4 + dy)
                total += yred[4 + dy].astype(f32)
            zsend[...] = total.astype(bf16)
            z_sum.start()

        return carry

    lax.fori_loop(0, 16, second, 0)
    total = acc[0] + diagonal(1)
    finish_rows(1)
    for dy in (1, 2, 3):
        got2(dy)
        total += yred[dy].astype(f32)
    z_sum.wait_recv()
    total += zred[...].astype(f32)
    dk_out[...] = total[:, :head].astype(bf16)
    dv_out[...] = total[:, head:].astype(bf16)

    for copy in grads + kv_copies:
        copy.wait_send()
    for j in (1, 2, 3, 9, 10, 11):
        forward(j).wait_send()
    for n in range(8):
        sum1(n).wait_send()
        if n % 4:
            sum2(n).wait_send()
    z_sum.wait_send()


def body(queries, keys, values, outputs, grad_held, lse, span_start):
    tokens, heads, head = queries.shape[1:]
    n = lax.axis_size("ctx")
    rows = tokens * heads // 2
    vm = pl.BlockSpec(memory_space=pltpu.VMEM)
    hbm = pl.BlockSpec(memory_space=pl.ANY)
    dma = pltpu.SemaphoreType.DMA
    tile = (tokens, 2 * head)
    dq, dk, dv = pl.pallas_call(
        kernel,
        out_shape=(
            jax.ShapeDtypeStruct((2 * rows, head), bf16),
            jax.ShapeDtypeStruct((tokens, head), bf16),
            jax.ShapeDtypeStruct((tokens, head), bf16),
        ),
        in_specs=[pl.BlockSpec(memory_space=pltpu.SMEM)] + [hbm] * 6,
        out_specs=(vm, vm, vm),
        scratch_shapes=[
            pltpu.VMEM((rows, 2 * head), bf16),
            pltpu.VMEM((rows, 2 * head), bf16),
            pltpu.VMEM((rows, 2 * head), bf16),
            pltpu.VMEM((heads, tokens), f32),
            pltpu.VMEM((n, *tile), bf16),
            pltpu.VMEM((2 * head, rows), f32),
            pltpu.VMEM((2, 1, rows), f32),
            pltpu.VMEM((2, 1, rows), f32),
            pltpu.VMEM((n, *tile), f32),
            pltpu.VMEM((8, *tile), bf16),
            pltpu.VMEM((8, *tile), bf16),
            pltpu.VMEM((8, *tile), bf16),
            pltpu.VMEM((8, *tile), bf16),
            pltpu.VMEM(tile, bf16),
            pltpu.VMEM(tile, bf16),
            dma((7,)), dma((4,)), dma((4,)), dma((9,)), dma((16,)), dma((12,)),
            dma((8,)), dma((8,)), dma((8,)), dma((8,)), dma((1,)), dma((1,)),
        ],
        compiler_params=pltpu.CompilerParams(
            vmem_limit_bytes=60 << 20, collective_id=0, has_side_effects=True
        ),
    )(
        span_start,
        queries.reshape(2 * rows, head),
        keys[0],
        values[0],
        grad_held.reshape(2 * rows, head),
        outputs.reshape(2 * rows, head),
        lse[0],
    )
    return dq.reshape(1, tokens, heads, head), dk[None], dv[None]


def solution(mesh):
    rows = P("section", "ctx", None, None)
    keys = P("section", "ctx", None)
    return jax.shard_map(
        body,
        mesh=mesh,
        in_specs=(rows, keys, keys, rows, rows, P("section", None, "ctx"), P()),
        out_specs=(rows, keys, keys),
        check_vma=False,
    )
```

```python
import jax
import jax.numpy as jnp
from jax import lax
from jax.experimental import pallas as pl
from jax.experimental.pallas import tpu as pltpu
from jax.sharding import PartitionSpec as P

bf16, f32 = jnp.bfloat16, jnp.float32
LOG2E = 1.4426950408889634
FAR = 1e30
MESH = pl.DeviceIdType.MESH
PHASES = 2
CUT = 6


def nn(a, b):
    return lax.dot_general(a, b, (((1,), (0,)), ((), ())), preferred_element_type=f32)


def nt(a, b):
    return lax.dot_general(a, b, (((1,), (1,)), ((), ())), preferred_element_type=f32)


def pair(top_left, top_right, bottom_left, bottom_right):
    top = jnp.concatenate([top_left, top_right], 1)
    return jnp.concatenate([top, jnp.concatenate([bottom_left, bottom_right], 1)], 0)


def attend(key_pair, value_pair, lse_pair, delta_pair, mask, rows, qc, dc, dq):
    span = key_pair.shape[0] // 2
    scale2 = (key_pair.shape[1] // 2) ** -0.5 * LOG2E
    scores = nt(key_pair, qc[rows, :]) * scale2
    grads = nt(value_pair, dc[rows, :])
    probs, terms = [], []
    for slot in range(2):
        part = slice(slot * span, (slot + 1) * span)
        prob = jnp.exp2(scores[part] - lse_pair[slot])
        if mask is not None:
            prob = jnp.where(mask, prob, 0.0)
        probs.append(prob)
        terms.append(prob * (grads[part] - delta_pair[slot]))
    probs = jnp.concatenate(probs, 0).astype(bf16)
    terms = jnp.concatenate(terms, 0).astype(bf16)
    dq[:, rows] += nn(key_pair.T, terms)
    return nn(terms, qc[rows, :]), nn(probs, dc[rows, :])


def kernel(
    starts, q, k, v, g, o, lse, dq_out, dk_out, dv_out,
    qc, dc, ob, lb, kv, dq, lse_rows, delta, acc, cred, send1, send2, yred, zsend, zred,
    in_s, grad_s, grad_r, kv_s, kv_r, fwd_s, s1_s, s1_r, s2_s, s2_r, z_s, z_r,
):
    me, sec = lax.axis_index("ctx"), lax.axis_index("section")
    sections = lax.axis_size("section")
    half_rows, head = qc.shape[0], qc.shape[1] // 2
    span = kv.shape[1] // 2
    scale = head ** -0.5
    edges = (0, half_rows * CUT // 16, half_rows)
    zh, y, core = me // 8, (me // 2) % 4, me % 2

    def at(dz, dy, dc):
        return (((zh + dz) % 2) * 4 + (y + dy) % 4) * 2 + (core + dc) % 2

    def index_of(j):
        return at(j // 8, j % 4, (j // 4) % 2)

    def remote(src, dst, send, recv, target):
        return pltpu.make_async_remote_copy(
            src_ref=src, dst_ref=dst, send_sem=send, recv_sem=recv,
            device_id=target, device_id_type=MESH,
        )

    core_peer, z_peer = {"ctx": at(0, 0, 1)}, {"ctx": at(1, 0, 0)}
    y_peers = [{"ctx": at(0, dy, 0)} for dy in (1, 2, 3)]
    before = {"section": (sec + sections - 1) % sections}
    after = {"section": (sec + 1) % sections}

    def rows_of(phase):
        return pl.ds(edges[phase], edges[phase + 1] - edges[phase])

    local = [
        pltpu.make_async_copy(k, kv.at[me, :, pl.ds(0, head)], in_s.at[0]),
        pltpu.make_async_copy(v, kv.at[me, :, pl.ds(head, head)], in_s.at[1]),
        pltpu.make_async_copy(lse, lb, in_s.at[2]),
    ]
    for half in range(2):
        part, cols = pl.ds(half * half_rows, half_rows), pl.ds(half * head, head)
        local.append(pltpu.make_async_copy(q.at[part, :], qc.at[:, cols], in_s.at[3 + half]))
        local.append(pltpu.make_async_copy(o.at[part, :], ob.at[:, cols], in_s.at[5 + half]))
    for copy in local:
        copy.start()

    barrier = pltpu.get_barrier_semaphore()
    peers = [core_peer, z_peer, *y_peers, before, after]
    for peer in peers:
        pl.semaphore_signal(barrier, inc=1, device_id=peer, device_id_type=MESH)
    pl.semaphore_wait(barrier, len(peers))

    for copy in local[:2]:
        copy.wait()

    def spread(shard, base, first):
        out = []
        for n, (peer, slot) in enumerate(
            [(y_peers[0], 3), (y_peers[2], 1), (y_peers[1], 2), (core_peer, 4)]
        ):
            out.append(
                remote(kv.at[shard], kv.at[shard], kv_s.at[base + n], kv_r.at[first + slot], peer)
            )
        return out

    def arrived(j):
        spot = kv.at[index_of(j)]
        remote(spot, spot, kv_s.at[0], kv_r.at[j], core_peer).wait_recv()

    def forward(j):
        spot = kv.at[index_of(j)]
        return remote(spot, spot, fwd_s.at[j], kv_r.at[j + 4], core_peer)

    z_copy = remote(kv.at[me], kv.at[me], kv_s.at[8], kv_r.at[8], z_peer)
    grads = []
    for phase in range(PHASES):
        for half in range(2):
            n = phase * 2 + half
            grads.append(
                remote(
                    g.at[pl.ds(half * half_rows + edges[phase], edges[phase + 1] - edges[phase]), :],
                    dc.at[rows_of(phase), pl.ds(half * head, head)],
                    grad_s.at[n], grad_r.at[n], before,
                )
            )
            grads[-1].start()
        if phase == 0:
            z_copy.start()
    kv_copies = [*spread(me, 0, 0)]
    for copy in kv_copies:
        copy.start()
    kv_copies += [z_copy, *spread(index_of(8), 4, 8)]

    dq[...] = jnp.zeros_like(dq)
    for copy in local[2:]:
        copy.wait()
    lane = lax.broadcasted_iota(jnp.int32, (16, 128), 1)
    pick = jnp.where(lane % 16 == lax.broadcasted_iota(jnp.int32, (16, 128), 0), 1.0, 0.0).astype(f32)
    tokens = lax.broadcasted_iota(jnp.int32, (128, 128), 0)
    lanes = lax.broadcasted_iota(jnp.int32, (128, 128), 1)
    for half in range(2):
        part = lb[:, half * 128 : (half + 1) * 128] * LOG2E
        wide = lax.dot_general(
            part, pick, (((0,), (0,)), ((), ())),
            precision=lax.Precision.HIGHEST, preferred_element_type=f32,
        )
        wide = jnp.where(lanes // 16 == tokens % 8, wide, 0.0)
        packed = jnp.sum(wide.reshape(16, 8, 128), axis=1)
        for i in range(16):
            lse_rows[half, :, i * 128 : (i + 1) * 128] = packed[i : i + 1]

    for j in (1, 3, 2):
        arrived(j)
        forward(j).start()

    zero = jnp.zeros((span, head), bf16)
    low_start = starts[2 * me]
    ones = jnp.ones((8, head), bf16)

    def start_phase(phase):
        rows = rows_of(phase)
        for half in range(2):
            grads[phase * 2 + half].wait_recv()
        for half in range(2):
            cols = pl.ds(half * head, head)
            prod = dc[rows, cols].astype(f32) * ob[rows, cols].astype(f32)
            high = prod.astype(bf16)
            low = (prod - high.astype(f32)).astype(bf16)
            delta[half, :, rows] = (nt(ones, high) + nt(ones, low))[:1]

    def diagonal(phase):
        rows = rows_of(phase)
        token = lax.shift_right_logical(
            lax.broadcasted_iota(jnp.int32, (span, rows.size), 1), (half_rows // span).bit_length() - 1
        ) + edges[phase] * span // half_rows
        mask = lax.broadcasted_iota(jnp.int32, (span, rows.size), 0) <= token
        k_a, k_b = kv[me, :span, :head], kv[me, span:, :head]
        v_a, v_b = kv[me, :span, head:], kv[me, span:, head:]
        dk, dv = attend(
            pair(zero, k_b, k_a, zero),
            pair(zero, v_b, v_a, zero),
            (lse_rows[1, :, rows], lse_rows[0, :, rows]),
            (delta[1, :, rows], delta[0, :, rows]),
            mask, rows, qc, dc, dq,
        )
        dk *= scale
        return pair(dk[span:, :head], dv[span:, :head], dk[:span, head:], dv[:span, head:])

    def shard_terms(j, phase):
        rows = rows_of(phase)
        m = index_of(j)
        sel = starts[2 * m] < low_start
        on = jnp.where(sel, 1.0, 0.0).astype(f32)
        off = 1.0 - on
        lse_a, lse_b = lse_rows[0, :, rows], lse_rows[1, :, rows]
        del_a, del_b = delta[0, :, rows], delta[1, :, rows]
        k_a, k_b = kv[m, :span, :head], kv[m, span:, :head]
        v_a, v_b = kv[m, :span, head:], kv[m, span:, head:]
        dk, dv = attend(
            pair(zero, k_a, (k_a * on).astype(bf16), (k_b * off).astype(bf16)),
            pair(zero, v_a, (v_a * on).astype(bf16), (v_b * off).astype(bf16)),
            (lse_b, jnp.where(j == 0, FAR, jnp.where(sel, lse_a, lse_b))),
            (del_b, jnp.where(sel, del_a, del_b)),
            None, rows, qc, dc, dq,
        )
        dk *= scale
        return pair(
            dk[:span, head:] + on * dk[span:, :head],
            dv[:span, head:] + on * dv[span:, :head],
            off * dk[span:, head:],
            off * dv[span:, head:],
        )

    def finish_rows(phase):
        for half in range(2):
            low, high = edges[phase], edges[phase + 1]
            part = dq[half * head : (half + 1) * head, low:high]
            dq_out[pl.ds(half * half_rows + low, high - low), :] = (part.T * scale).astype(bf16)

    start_phase(0)
    acc[0] = diagonal(0)

    def first(j, carry):
        waits = jnp.logical_or(j // 4 == 1, j >= 9)

        @pl.when(waits)
        def _():
            arrived(j)

        @pl.when(jnp.logical_and(j >= 9, j < 12))
        def _():
            forward(j).start()

        @pl.when(j == 4)
        def _():
            arrived(8)
            for copy in spread(index_of(8), 4, 8):
                copy.start()

        terms = shard_terms(j, 0)

        @pl.when(j == 0)
        def _():
            acc[0] += terms

        @pl.when(j > 0)
        def _():
            acc[j] = terms

        return carry

    lax.fori_loop(0, 16, first, 0)
    finish_rows(0)
    start_phase(1)

    def sum1(n):
        return remote(send1.at[n], cred.at[n], s1_s.at[n], s1_r.at[n], core_peer)

    def sum2(n):
        dy = n % 4
        back = (n // 4) * 4 + (4 - dy) % 4
        return remote(
            send2.at[n], yred.at[back], s2_s.at[n], s2_r.at[back], {"ctx": at(0, dy, 0)}
        )

    def got2(n):
        remote(send2.at[n], yred.at[n], s2_s.at[n], s2_r.at[n], core_peer).wait_recv()

    z_sum = remote(zsend, zred, z_s.at[0], z_r.at[0], z_peer)

    def second(i, carry):
        j = 15 - i
        n = (j // 8) * 4 + j % 4
        terms = acc[j] + shard_terms(j, 1)
        kept = (j // 4) % 2 == 0

        @pl.when(jnp.logical_not(kept))
        def _():
            send1[n] = terms.astype(bf16)
            sum1(n).start()

        @pl.when(kept)
        def _():
            sum1(n).wait_recv()
            total = terms + cred[n].astype(f32)

            @pl.when(j % 4 == 0)
            def _():
                acc[j] = total

            @pl.when(j % 4 != 0)
            def _():
                send2[n] = total.astype(bf16)
                sum2(n).start()

        @pl.when(j == 5)
        def _():
            total = acc[8]
            for dy in (1, 2, 3):
                got2(4 + dy)
                total += yred[4 + dy].astype(f32)
            zsend[...] = total.astype(bf16)
            z_sum.start()

        return carry

    lax.fori_loop(0, 16, second, 0)
    total = acc[0] + diagonal(1)
    finish_rows(1)
    for dy in (1, 2, 3):
        got2(dy)
        total += yred[dy].astype(f32)
    z_sum.wait_recv()
    total += zred[...].astype(f32)
    dk_out[...] = total[:, :head].astype(bf16)
    dv_out[...] = total[:, head:].astype(bf16)

    for copy in grads + kv_copies:
        copy.wait_send()
    for j in (1, 2, 3, 9, 10, 11):
        forward(j).wait_send()
    for n in range(8):
        sum1(n).wait_send()
        if n % 4:
            sum2(n).wait_send()
    z_sum.wait_send()


def hand_over(dq, dk, dv, dq_out, dk_out, dv_out):
    dq_out[...] = dq[...]
    dk_out[...] = dk[...]
    dv_out[...] = dv[...]


def body(queries, keys, values, outputs, grad_held, lse, span_start):
    tokens, heads, head = queries.shape[1:]
    n = lax.axis_size("ctx")
    rows = tokens * heads // 2
    vm = pl.BlockSpec(memory_space=pltpu.VMEM)
    hbm = pl.BlockSpec(memory_space=pl.ANY)
    dma = pltpu.SemaphoreType.DMA
    tile = (tokens, 2 * head)
    dq, dk, dv = pl.pallas_call(
        kernel,
        out_shape=(
            jax.ShapeDtypeStruct((2 * rows, head), bf16),
            jax.ShapeDtypeStruct((tokens, head), bf16),
            jax.ShapeDtypeStruct((tokens, head), bf16),
        ),
        in_specs=[pl.BlockSpec(memory_space=pltpu.SMEM)] + [hbm] * 6,
        out_specs=(vm, vm, vm),
        scratch_shapes=[
            pltpu.VMEM((rows, 2 * head), bf16),
            pltpu.VMEM((rows, 2 * head), bf16),
            pltpu.VMEM((rows, 2 * head), bf16),
            pltpu.VMEM((heads, tokens), f32),
            pltpu.VMEM((n, *tile), bf16),
            pltpu.VMEM((2 * head, rows), f32),
            pltpu.VMEM((2, 1, rows), f32),
            pltpu.VMEM((2, 1, rows), f32),
            pltpu.VMEM((n, *tile), f32),
            pltpu.VMEM((8, *tile), bf16),
            pltpu.VMEM((8, *tile), bf16),
            pltpu.VMEM((8, *tile), bf16),
            pltpu.VMEM((8, *tile), bf16),
            pltpu.VMEM(tile, bf16),
            pltpu.VMEM(tile, bf16),
            dma((7,)), dma((4,)), dma((4,)), dma((9,)), dma((16,)), dma((12,)),
            dma((8,)), dma((8,)), dma((8,)), dma((8,)), dma((1,)), dma((1,)),
        ],
        compiler_params=pltpu.CompilerParams(
            vmem_limit_bytes=60 << 20, collective_id=0, has_side_effects=True
        ),
    )(
        span_start,
        queries.reshape(2 * rows, head),
        keys[0],
        values[0],
        grad_held.reshape(2 * rows, head),
        outputs.reshape(2 * rows, head),
        lse[0],
    )
    parts = 4
    big = pl.BlockSpec((2 * rows // parts, head), lambda i: (i, 0))
    small = pl.BlockSpec((tokens // parts, head), lambda i: (i, 0))
    dq, dk, dv = pl.pallas_call(
        hand_over,
        grid=(parts,),
        out_shape=tuple(jax.ShapeDtypeStruct(x.shape, x.dtype) for x in (dq, dk, dv)),
        in_specs=[big, small, small],
        out_specs=(big, small, small),
    )(dq, dk, dv)
    return dq.reshape(1, tokens, heads, head), dk[None], dv[None]


def solution(mesh):
    rows = P("section", "ctx", None, None)
    keys = P("section", "ctx", None)
    return jax.shard_map(
        body,
        mesh=mesh,
        in_specs=(rows, keys, keys, rows, rows, P("section", None, "ctx"), P()),
        out_specs=(rows, keys, keys),
        check_vma=False,
    )
```
